32 devices in a mesh: node: 8 (over z, core), local: 4 (over y, x).
Axes of the slice: x: 2, y: 2, z: 4, core: 2. Of those that a mesh axis runs over, the one named last changes fastest.
Arguments:
- tokens: bfloat16 [64, 7168], P(('node', 'local')), may hold values from -6 to 6
- expert_ids: int32 [64, 8], P(('node', 'local')), may hold values from 0 to 31, all different within a row; in each aligned block of 8 rows (0 to 7, 8 to 15, ...) at most 4 rows name the same one
- gate_weights: bfloat16 [64, 8], P(('node', 'local')), may hold values from 0.049804688 to 1
- expert_seeds: int32 [32], P('node'), may hold values from 0 to 16777215
Outputs:
- moe_out: bfloat16 [64, 7168], P(('node', 'local'))
The draws below stay inside these ranges and needn't reach their ends.
Inputs may be any that keep to these rules, and one draw needn't show every extreme that they name: `expert_ids`: each row names 8 different experts. Within the tokens of one node group (aligned blocks of 8 rows), no expert is named by more than 4 rows, a bound that some block reaches.
All inputs are finite; a program needn't handle non-finite values.
Results may differ from the reference program's by a relative error of at most 0.0078.
Values may be sent and summed in bfloat16 or wider, within the bound.
No kernel may reach another device: no remote copies, remote signals or barrier semaphores. Data moves between devices by JAX's collectives and lax.ppermute only.
A program may use at most 128 MiB of HBM per device.

```python
import math
import jax
import jax.numpy as jnp
import numpy as np
from jax import lax

D = 7168
FF = 2048
TOP = 8
EXP_NODE = 4
TOK_NODE = 8
TOKENS = 64
EXPERTS = 32
CAPN = 4
N_NODE = 8
N_LOCAL = 4


def plant(values, own_key, smallest, top_value):
    longest = values.shape.index(max(values.shape))
    spots = []
    for shift in (0, 1):
        where = [jax.random.randint(jax.random.fold_in(own_key, axis), (), 0, length) for axis, length in enumerate(values.shape)]
        where[longest] = (where[longest] + shift) % values.shape[longest]
        spots.append(tuple(where))
    return values.at[spots[0]].set(smallest).at[spots[1]].set(top_value)


def shard_levels(rng, shape, cuts, least, top_value):
    level = 1.0
    for position, shards_of in cuts:
        draws = jax.random.uniform(jax.random.fold_in(jax.random.fold_in(rng, 6), position), (shards_of,), jnp.float32, least / len(cuts), top_value / len(cuts))
        level = level * jnp.repeat(jnp.exp(draws), shape[position] // shards_of).reshape((-1,) + (1,) * (len(shape) - 1 - position))
    return level


def deal_out(key, own, number, rows, count, top, limit, slope):
    sequence = jax.random.permutation(key, count)
    heavy_load, ordinary = shares(count, rows * top, limit, slope, True), shares(count, rows * top, limit, slope, False)
    places = jnp.arange(count)

    def named(sizes, rotation):
        used = int((sizes > 0).sum())
        fixed = max(1, used // 4)
        passed = fixed + (places - fixed + rotation * (used - fixed)) % max(1, count - fixed)
        return jnp.zeros((count,), jnp.int32).at[sequence[jnp.where(places < fixed, places, passed)]].set(jnp.asarray(sizes, jnp.int32))

    sizes = jnp.where(number % 4 == 0, named(heavy_load, number // 4), named(ordinary, number - number // 4 - 1))
    mixed = jax.random.permutation(jax.random.fold_in(own, 3), count)
    giver, sink = mixed[0:count // 2 * 2:2], mixed[1:count // 2 * 2:2]
    margin = jnp.minimum(sizes[giver] - 1, limit - sizes[sink]) // 2
    margin = jnp.where((giver == sequence[0]) | (sink == sequence[0]) | (sizes[sink] == 0), 0, jnp.maximum(margin, 0))
    passed = jax.random.randint(jax.random.fold_in(own, 4), (count // 2,), 0, 1 << 20) % (margin + 1)
    sizes = sizes.at[giver].add(-passed).at[sink].add(passed)
    members = jnp.searchsorted(jnp.cumsum(sizes), jnp.arange(rows * top), side="right").astype(jnp.int32)
    table = members.reshape(top, rows).T
    table = table[jax.random.permutation(jax.random.fold_in(own, 1), rows)]
    rotation = jax.random.randint(jax.random.fold_in(own, 2), (rows, 1), 0, top)
    return jnp.take_along_axis(table, (jnp.arange(top)[None, :] + rotation) % top, axis=1)


def shares(count, total, reach, slope, full):
    portions = [(1 << 20) // math.isqrt(standing ** slope) + 1 for standing in range(1, count + 1)]
    largest = reach if full else min(reach, max(-(-total // count), total * portions[0] // sum(portions)))
    least = 1 if total - largest >= count - 1 else 0
    holding, spare = [largest] + [least] * (count - 1), total - largest - least * (count - 1)
    while spare > 0:
        free = [i for i in range(1, count) if holding[i] < largest] or [i for i in range(1, count) if holding[i] < reach]
        whole, budget = sum([portions[i] for i in free]), spare
        for i in free:
            extra = min(reach - holding[i], max(1, budget * portions[i] // whole), spare)
            holding[i] = holding[i] + extra
            spare = spare - extra
    return np.array(holding)


def bell_draw(own_key, dims, deviation, bound, split=(), kind=jnp.bfloat16):
    values = jax.random.normal(own_key, dims, jnp.float32) * deviation
    if len(split) > 0:
        values = shard_levels(own_key, dims, split, -0.22, 0.18) * values
    return jnp.clip(values, min=-bound, max=bound).astype(kind)


def setup_inputs(seed: int = 0) -> dict:
    key_list = jax.random.split(jax.random.key(seed), 5)
    tokens = bell_draw(key_list[0], (TOKENS, D), 1.0, 6.0, ((0, 32),))
    expert_ids_keys = jax.random.split(jax.random.fold_in(key_list[1], 1), TOKENS // TOK_NODE)
    expert_ids_turns = jax.random.permutation(jax.random.fold_in(key_list[1], 3), TOKENS // TOK_NODE)
    expert_ids = jax.vmap(lambda own, number: deal_out(jax.random.fold_in(key_list[1], 2), own, number, TOK_NODE, EXPERTS, TOP, CAPN, 2))(expert_ids_keys, expert_ids_turns).reshape((TOKENS, TOP))
    gate_weights = jnp.clip(jnp.exp(math.log(1.0) - 2.9996462 * jax.random.uniform(key_list[2], (TOKENS, TOP), jnp.float32) ** shard_levels(key_list[2], (TOKENS, TOP), ((0, 32),), -0.2, 0.2)), 0.049804688, 1.0).astype(jnp.bfloat16)
    expert_seeds = plant(jax.random.randint(key_list[3], (EXPERTS,), 0, 16777216), jax.random.fold_in(key_list[3], 1), 0, 16777215).astype(jnp.int32)
    return {"tokens": tokens, "expert_ids": expert_ids, "gate_weights": gate_weights, "expert_seeds": expert_seeds}


mix_const = 73244475

def hashed_weights(expert_seed, matrix_code, row_ids, col_ids, col_count, fan_in):
    flat_index = row_ids[:, None] * col_count + col_ids[None, :]
    mixing = expert_seed + matrix_code * 1000003 + flat_index * 374761393
    mixing = mixing ^ jnp.right_shift(mixing, 16)
    mixing = mixing * mix_const
    mixing = mixing ^ jnp.right_shift(mixing, 15)
    mixing = mixing * mix_const
    mixing = mixing ^ jnp.right_shift(mixing, 16)
    uniform_part = (mixing & 16777215).astype(jnp.float32) * (1.0 / 16777216.0) - 0.5
    return (uniform_part * math.sqrt(12.0 / fan_in)).astype(jnp.bfloat16)

def expert_rows(row_block, expert_seed, first_unit, unit_count, hidden_block, hidden_total):
    model_width = row_block.shape[1]
    feature_ids = jnp.arange(model_width, dtype=jnp.int32)
    accumulated = jnp.zeros((row_block.shape[0], model_width), jnp.float32)
    for offset in range(0, unit_count, hidden_block):
        hidden_ids = first_unit + offset + jnp.arange(hidden_block, dtype=jnp.int32)
        gate_and_up = jnp.concatenate([hashed_weights(expert_seed, 0, feature_ids, hidden_ids, hidden_total, model_width), hashed_weights(expert_seed, 1, feature_ids, hidden_ids, hidden_total, model_width)], axis=1)
        w_down = hashed_weights(expert_seed, 2, hidden_ids, feature_ids, model_width, hidden_total)
        projected = jnp.dot(row_block, gate_and_up, preferred_element_type=jnp.float32)
        hidden = (jax.nn.silu(projected[:, :hidden_block]) * projected[:, hidden_block:]).astype(jnp.bfloat16)
        accumulated = accumulated + jnp.dot(hidden, w_down, preferred_element_type=jnp.float32)
    return accumulated.astype(jnp.bfloat16)

def reference(tokens, expert_ids, gate_weights, expert_seeds):
    quarters = N_LOCAL // EXP_NODE
    quarter_width = FF // quarters
    hidden_block = min(quarter_width, 256)
    slot_total = N_NODE * CAPN
    gate_values = gate_weights.astype(jnp.float32)

    def one_expert(accumulated, expert):
        chosen = expert_ids == expert
        weight = lax.optimization_barrier(jnp.sum(jnp.where(chosen, gate_values, 0.0), axis=1))
        routed = jnp.any(chosen, axis=1)
        packing = jnp.argsort(jnp.where(routed, 0, 1).astype(jnp.int32), stable=True)[:slot_total].astype(jnp.int32)
        picked_rows = tokens[packing]
        token_scale = jnp.where(routed[packing], weight[packing], 0.0)
        expert_seed = expert_seeds[expert]
        output = jnp.zeros((slot_total, D), jnp.float32)
        for quarter in range(quarters):
            quarter_part = expert_rows(picked_rows, expert_seed, quarter * quarter_width, quarter_width, hidden_block, FF)
            output = output + quarter_part.astype(jnp.float32)
        accumulated = accumulated.at[packing].add(token_scale[:, None] * output)
        return (accumulated, None)
    accumulated, _ = lax.scan(one_expert, jnp.zeros((TOKENS, D), jnp.float32), jnp.arange(EXPERTS, dtype=jnp.int32))
    return accumulated.astype(jnp.bfloat16)
```

```python
import math

import jax
import jax.numpy as jnp
from jax import lax
from jax.experimental import pallas as pl
from jax.experimental.pallas import tpu as pltpu
from jax.sharding import PartitionSpec as P

FF = 2048
TOP = 8
EXP_NODE = 4

STEP = 374761393
MIX = 73244475
CODE = 1000003
LANES = 128
BLOCK = 256
HALF = float(1 << 23)


def wrap(value):
    value &= 0xFFFFFFFF
    return value - (1 << 32) if value >= 1 << 31 else value


def mixed(v):
    v = v ^ (v >> 16)
    v = v * MIX
    v = v ^ (v >> 15)
    v = v * MIX
    v = v ^ (v >> 16)
    return (v & 16777215).astype(jnp.float32).astype(jnp.bfloat16)


def index_table(t_ref, row_stride):
    row = lax.broadcasted_iota(jnp.int32, t_ref.shape, 0)
    col = lax.broadcasted_iota(jnp.int32, t_ref.shape, 1)
    t_ref[...] = (row * row_stride + col) * STEP


def gate_up_tile(w_ref, table, base, rows, row_stride):
    for r in range(0, rows, 16):
        for c in range(2):
            word = table + (base + wrap(r * row_stride * STEP + c * CODE))
            w_ref[r : r + 16, c * BLOCK : (c + 1) * BLOCK] = mixed(word)


def down_tile(w_ref, table, bases, first_row, rows, source_rows, row_stride):
    for r in range(0, rows, 16):
        source, unit = divmod(first_row + r, source_rows)
        word = table + (bases[source] + wrap(unit * row_stride * STEP))
        w_ref[r : r + 16, :] = mixed(word)


def params(vmem=60 << 20):
    return pltpu.CompilerParams(vmem_limit_bytes=vmem)


def smem():
    return pl.BlockSpec(memory_space=pltpu.SMEM)


def estimate(elements, rows):
    return pl.CostEstimate(flops=40 * elements + 2 * rows * elements, bytes_accessed=2 * elements, transcendentals=0)


def early_gate_up(scalars, pre_rows, blocks, hidden_total):
    half = pre_rows // 2

    def kernel(s_ref, w_ref, t_ref):
        block, part = pl.program_id(0), pl.program_id(1)
        index_table(t_ref, hidden_total)
        base = s_ref[0] + (s_ref[1] + block * BLOCK + part * (half * hidden_total)) * STEP
        gate_up_tile(w_ref.at[0], t_ref[...], base, half, hidden_total)

    return pl.pallas_call(
        kernel,
        grid=(blocks, 2),
        in_specs=[smem()],
        out_specs=pl.BlockSpec((1, half, 2 * BLOCK), lambda b, p: (b, p, 0)),
        out_shape=jax.ShapeDtypeStruct((blocks, pre_rows, 2 * BLOCK), jnp.bfloat16),
        scratch_shapes=[pltpu.VMEM((16, BLOCK), jnp.int32)],
        compiler_params=params(),
        cost_estimate=estimate(blocks * pre_rows * 2 * BLOCK, 0),
        name="early_gate_up",
    )(scalars)


def hidden_rows(scalars, rows, row_weight, early, model_width, hidden_total):
    blocks, pre_rows, _ = early.shape
    count = rows.shape[0]
    half = (model_width - pre_rows) // 2
    scale = math.sqrt(12.0 / model_width) / 16777216.0

    def kernel(s_ref, x_ref, g_ref, early_ref, h_ref, t_ref, wa, wb, shift_ref):
        block = pl.program_id(0)

        def make(step, first_row, w_ref):
            base = s_ref[0] + (s_ref[1] + step * BLOCK + first_row * hidden_total) * STEP
            gate_up_tile(w_ref, t_ref[...], base, half, hidden_total)

        @pl.when(block == 0)
        def _():
            index_table(t_ref, hidden_total)
            total = jnp.sum(x_ref[:, :model_width].astype(jnp.float32), axis=1, keepdims=True)
            shift_ref[...] = jnp.broadcast_to(total * HALF, shift_ref.shape)
            make(0, pre_rows, wa)

        def times(first_row, length, w):
            return jnp.dot(x_ref[:, first_row : first_row + length], w, preferred_element_type=jnp.float32)

        total = times(0, pre_rows, early_ref[0])
        total = total + times(pre_rows, half, wa[...])
        make(block, pre_rows + half, wb)
        total = total + times(pre_rows + half, half, wb[...])
        make(block + 1, pre_rows, wa)
        total = (total - shift_ref[:, :1]) * scale
        gate, up = total[:, :BLOCK], total[:, BLOCK:]
        h_ref[...] = (gate * jax.nn.sigmoid(gate) * up * g_ref[...]).astype(jnp.bfloat16)

    vmem = pl.BlockSpec(memory_space=pltpu.VMEM)
    return pl.pallas_call(
        kernel,
        grid=(blocks,),
        in_specs=[smem(), vmem, vmem, pl.BlockSpec((1, pre_rows, 2 * BLOCK), lambda b: (b, 0, 0))],
        out_specs=pl.BlockSpec((count, BLOCK), lambda b: (0, b)),
        out_shape=jax.ShapeDtypeStruct((count, blocks * BLOCK), jnp.bfloat16),
        scratch_shapes=[
            pltpu.VMEM((16, BLOCK), jnp.int32),
            pltpu.VMEM((half, 2 * BLOCK), jnp.bfloat16),
            pltpu.VMEM((half, 2 * BLOCK), jnp.bfloat16),
            pltpu.VMEM((count, LANES), jnp.float32),
        ],
        compiler_params=params(),
        cost_estimate=estimate(blocks * 2 * half * 2 * BLOCK, count),
        name="hidden_rows",
    )(scalars, rows, row_weight, early)


def early_down(scalars, pre_rows, source_rows, columns, model_width):
    sources = -(-pre_rows // source_rows)

    def kernel(s_ref, w_ref, t_ref):
        index_table(t_ref, model_width)
        column = pl.program_id(0) * wrap(BLOCK * STEP)
        bases = [s_ref[i] + column for i in range(sources)]
        down_tile(w_ref.at[0], t_ref[...], bases, 0, pre_rows, source_rows, model_width)

    return pl.pallas_call(
        kernel,
        grid=(columns // BLOCK,),
        in_specs=[smem()],
        out_specs=pl.BlockSpec((1, pre_rows, BLOCK), lambda b: (b, 0, 0)),
        out_shape=jax.ShapeDtypeStruct((columns // BLOCK, pre_rows, BLOCK), jnp.bfloat16),
        scratch_shapes=[pltpu.VMEM((16, BLOCK), jnp.int32)],
        compiler_params=params(),
        cost_estimate=estimate(columns * pre_rows, 0),
        name="early_down",
    )(scalars)


def output_rows(scalars, hidden, early, source_rows, hidden_total, model_width):
    blocks, pre_rows, _ = early.shape
    count, depth = hidden.shape
    half = (depth - pre_rows) // 2
    sources = depth // source_rows
    scale = math.sqrt(12.0 / hidden_total) / 16777216.0

    def kernel(s_ref, h_ref, early_ref, o_ref, t_ref, wa, wb, shift_ref):
        block = pl.program_id(0)

        def make(step, first_row, w_ref):
            column = step * wrap(BLOCK * STEP)
            bases = [s_ref[i] + column for i in range(sources)]
            down_tile(w_ref, t_ref[...], bases, first_row, half, source_rows, model_width)

        @pl.when(block == 0)
        def _():
            index_table(t_ref, model_width)
            total = jnp.sum(h_ref[...].astype(jnp.float32), axis=1, keepdims=True)
            shift_ref[...] = jnp.broadcast_to(total * HALF, shift_ref.shape)
            make(0, pre_rows, wa)

        def times(first_row, length, w):
            return jnp.dot(h_ref[:, first_row : first_row + length], w, preferred_element_type=jnp.float32)

        total = times(0, pre_rows, early_ref[0])
        total = total + times(pre_rows, half, wa[...])
        make(block, pre_rows + half, wb)
        total = total + times(pre_rows + half, half, wb[...])
        make(block + 1, pre_rows, wa)
        o_ref[...] = ((total - shift_ref[:, :1]) * scale).astype(jnp.bfloat16)

    vmem = pl.BlockSpec(memory_space=pltpu.VMEM)
    return pl.pallas_call(
        kernel,
        grid=(blocks,),
        in_specs=[smem(), vmem, pl.BlockSpec((1, pre_rows, BLOCK), lambda b: (b, 0, 0))],
        out_specs=pl.BlockSpec((count, BLOCK), lambda b: (0, b)),
        out_shape=jax.ShapeDtypeStruct((count, blocks * BLOCK), jnp.bfloat16),
        scratch_shapes=[
            pltpu.VMEM((16, BLOCK), jnp.int32),
            pltpu.VMEM((half, BLOCK), jnp.bfloat16),
            pltpu.VMEM((half, BLOCK), jnp.bfloat16),
            pltpu.VMEM((count, LANES), jnp.float32),
        ],
        compiler_params=params(),
        cost_estimate=estimate(blocks * 2 * half * BLOCK, count),
        name="output_rows",
    )(scalars, hidden, early)


def body(tokens, expert_ids, gate_weights, expert_seeds):
    n_node = lax.axis_size("node")
    n_local = lax.axis_size("local")
    devices = n_node * n_local
    quarters = n_local // EXP_NODE
    quarter_width = FF // quarters
    own_tokens, model_width = tokens.shape
    tok_node = own_tokens * n_local
    capacity = 2 * tok_node * TOP // (EXP_NODE * n_node)
    node_index = lax.axis_index("node")
    local_index = lax.axis_index("local")
    expert_kind = local_index // quarters
    first_unit = (local_index % quarters) * quarter_width
    blocks = quarter_width // BLOCK
    own_seed = expert_seeds[expert_kind]
    up_scalars = jnp.stack([own_seed, first_unit])
    early = early_gate_up(up_scalars, model_width // 2, blocks, FF)

    if devices * own_tokens <= 4 * n_node * capacity:
        pad = LANES - 2 * TOP
        packed = jnp.concatenate(
            [
                tokens,
                expert_ids.astype(jnp.bfloat16),
                gate_weights,
                jnp.zeros((own_tokens, pad), jnp.bfloat16),
            ],
            axis=1,
        )
        every = lax.all_to_all(
            jnp.broadcast_to(packed[None], (devices,) + packed.shape),
            ("node", "local"),
            split_axis=0,
            concat_axis=0,
            tiled=True,
        ).reshape(devices * own_tokens, model_width + LANES)
        routes = every[:, model_width : model_width + 2 * TOP].astype(jnp.float32)
        own_expert = (node_index * EXP_NODE + expert_kind).astype(jnp.float32)
        row_weight = jnp.sum(
            jnp.where(routes[:, :TOP] == own_expert, routes[:, TOP:], 0.0), axis=1, keepdims=True
        )
        hidden = hidden_rows(up_scalars, every, row_weight, early, model_width, FF)
        columns = model_width // n_local
        places = jnp.arange(n_local, dtype=jnp.int32)
        down_scalars = (
            jnp.repeat(expert_seeds, quarters)
            + 2 * CODE
            + ((places % quarters) * quarter_width * model_width + local_index * columns) * STEP
        )
        depth = n_local * quarter_width
        early_low = early_down(down_scalars, depth // 4, quarter_width, columns, model_width)
        shared = lax.all_to_all(
            jnp.broadcast_to(hidden[None], (n_local,) + hidden.shape),
            "local",
            split_axis=0,
            concat_axis=0,
            tiled=True,
        )
        stacked = jnp.transpose(shared, (1, 0, 2)).reshape(hidden.shape[0], depth)
        partial = output_rows(down_scalars, stacked, early_low, quarter_width, FF, model_width)
        returned = lax.all_to_all(
            partial.reshape(devices, own_tokens, columns),
            ("node", "local"),
            split_axis=0,
            concat_axis=0,
            tiled=True,
        )
        summed = jnp.sum(
            returned.reshape(n_node, n_local, own_tokens, columns).astype(jnp.float32), axis=0
        )
        return jnp.transpose(summed, (1, 0, 2)).reshape(own_tokens, model_width).astype(jnp.bfloat16)

    group_rows, group_ids, group_gates = (
        lax.all_gather(tokens, "local", axis=0, tiled=True),
        lax.all_gather(expert_ids, "local", axis=0, tiled=True),
        lax.all_gather(gate_weights, "local", axis=0, tiled=True),
    )
    targets = jnp.arange(n_node, dtype=jnp.int32) * EXP_NODE + expert_kind
    id_match = group_ids[:, :, None] == targets[None, None, :]
    routed = jnp.any(id_match, axis=1)
    picked = jnp.sum(jnp.where(id_match, group_gates.astype(jnp.float32)[:, :, None], 0.0), axis=1)
    place = jnp.where(routed, jnp.cumsum(routed.astype(jnp.int32), axis=0) - 1, -1)
    select = place.T[:, None, :] == jnp.arange(capacity, dtype=jnp.int32)[None, :, None]
    outgoing = jnp.einsum(
        "mct,td->mcd", select.astype(jnp.bfloat16), group_rows, preferred_element_type=jnp.float32
    ).astype(jnp.bfloat16)
    arrived = lax.all_to_all(outgoing, "node", split_axis=0, concat_axis=0, tiled=True)
    flat_rows = arrived.reshape(n_node * capacity, model_width)
    row_weight = jnp.ones((n_node * capacity, 1), jnp.float32)
    hidden = hidden_rows(up_scalars, flat_rows, row_weight, early, model_width, FF)
    down_scalars = (own_seed + 2 * CODE + first_unit * model_width * STEP)[None]
    early_low = early_down(down_scalars, quarter_width // 4, quarter_width, model_width, model_width)
    flat_out = output_rows(down_scalars, hidden, early_low, quarter_width, FF, model_width)
    returned = lax.all_to_all(
        flat_out.reshape(arrived.shape), "node", split_axis=0, concat_axis=0, tiled=True
    )
    combine = select.astype(jnp.float32) * picked.T[:, None, :]
    partial_term = jnp.einsum(
        "mct,mcd->td", combine, returned.astype(jnp.float32), precision=lax.Precision.HIGHEST
    )
    own_rows = lax.psum_scatter(partial_term, "local", scatter_dimension=0, tiled=True)
    return own_rows.astype(jnp.bfloat16)


def solution(mesh):
    return jax.shard_map(
        body,
        mesh=mesh,
        in_specs=(
            P(("node", "local"), None),
            P(("node", "local"), None),
            P(("node", "local"), None),
            P("node"),
        ),
        out_specs=P(("node", "local"), None),
        check_vma=False,
    )
```
